32 devices in a mesh: row: 4 (over y, x), col: 4 (over z), cores: 2 (over core).
Axes of the slice: x: 2, y: 2, z: 4, core: 2. Of those that a mesh axis runs over, the one named last changes fastest.
Arguments:
- multipoles: bfloat16 [315, 2048], P(None, ('col', 'row')), may hold values from -6 to 6
- operators: bfloat16 [40, 315, 315], P('cores'), may hold values from -0.0078125 to 0.0078125
- classes: int32 [2048, 2048], P('row', 'col'), may hold values from 0 to 39, as said below
- separated: int32 [4, 4], P('row', 'col'), may hold values 0 or 1
- owners: int32 [2048], P('row'), may hold values from 0 to 7, as said below
Outputs:
- owned: float32 [315, 4096], P(None, ('row', 'col', 'cores'))
The draws below stay inside these ranges and needn't reach their ends.
Inputs may be any that keep to these rules, and one draw needn't show every extreme that they name: `owners`: in each block of 512 cells (cells b * 512 to b * 512 + 511) no owner holds more than 128 cells, and in every block one owner holds exactly 128. Cell t sits at (t % 8, (t // 8) % 4, t // 32) on a periodic grid of 8 x 4 x 2048 // 32 cells; classes[t, s] depends only on the wrapped offset between the positions of t and s.
All inputs are finite; a program needn't handle non-finite values. No bound on the sum of `separated` on one device may be relied on, other than what follows from the above.
Results may differ from the reference program's by a relative error of at most 0.0029.
Values may be sent and summed in bfloat16 or wider, within the bound.
A program may use at most 64 MiB of HBM per device.

```python
import jax
import jax.numpy as jnp
from jax import lax

P_SIZE = 315
TB = 512
NC = 2048
NK = 40
GROUP = 8
CAP = 128
N_ROW = 4


def draw_owners(key, part):

    def one_block(sub):
        first, second, third = jax.random.split(sub, 3)
        full = jax.random.randint(first, (), 0, GROUP)
        slot_owner = jnp.arange(2 * TB, dtype=jnp.int32) // CAP
        score = jax.random.permutation(second, 2 * TB).astype(jnp.int32)
        score = jnp.where(slot_owner == full, score - 4 * TB, score)
        order = jnp.argsort(score, stable=True)
        chosen = slot_owner[order[:TB]]
        return jax.random.permutation(third, chosen)
    keys = jax.random.split(jax.random.fold_in(key, 7), NC // TB)
    return jax.vmap(one_block)(keys).reshape(-1).astype(jnp.int32)


def draw_classes(key, part):
    depth = NC // 32
    table = jax.random.randint(jax.random.fold_in(key, 11), (8 * 4 * depth,), 0, NK).astype(jnp.int32)
    cells = jnp.arange(NC, dtype=jnp.int32)
    xpos = cells % 8
    ypos = cells // 8 % 4
    zpos = cells // 32
    dx = (xpos[:, None] - xpos[None, :]) % 8
    dy = (ypos[:, None] - ypos[None, :]) % 4
    dz = (zpos[:, None] - zpos[None, :]) % depth
    offset = (dz * 4 + dy) * 8 + dx
    return table[offset].astype(jnp.int32)


def touch_ends(drawn, rng, low, high):
    longest = drawn.shape.index(max(drawn.shape))
    spots = []
    for shift in (0, 1):
        where = [jax.random.randint(jax.random.fold_in(rng, axis), (), 0, length) for axis, length in enumerate(drawn.shape)]
        where[longest] = (where[longest] + shift) % drawn.shape[longest]
        spots.append(tuple(where))
    return drawn.at[spots[0]].set(low).at[spots[1]].set(high)


def block_levels(rng, shape, shards, smallest, high):
    gain, own = 1.0, jax.random.fold_in(rng, 6)
    for axis_at, parts in shards:
        steps = jnp.exp(jax.random.uniform(jax.random.fold_in(own, axis_at), (parts,), jnp.float32, smallest / len(shards), high / len(shards)))
        gain = gain * jnp.repeat(steps, shape[axis_at] // parts).reshape([-1 if axis == axis_at else 1 for axis in range(len(shape))])
    return gain


def bell_draw(stream_key, dims, scale, bound, cuts=(), kind=jnp.bfloat16):
    factor_of = block_levels(stream_key, dims, cuts, -0.22, 0.18) if cuts else 1.0
    result = jax.random.normal(stream_key, dims, jnp.float32) * scale * factor_of
    return jnp.minimum(jnp.maximum(result, -bound), bound).astype(kind)


def setup_inputs(seed: int = 0) -> dict:
    seeds = jax.random.split(jax.random.key(seed), 6)
    multipoles = bell_draw(seeds[0], (P_SIZE, NC), 1.0, 6.0, ((1, 16),))
    operators = bell_draw(seeds[1], (NK, P_SIZE, P_SIZE), (P_SIZE * NC) ** -0.5, 0.0078125, ((0, 2),))
    classes = draw_classes(jax.random.fold_in(seeds[5], 71), 0)
    separated = touch_ends((jax.random.randint(seeds[3], (N_ROW, N_ROW), 0, 4) < 3).astype(jnp.int32), jax.random.fold_in(seeds[3], 1), 0, 1)
    owners = draw_owners(jax.random.fold_in(seeds[5], 71), 0)
    return dict(multipoles=multipoles, operators=operators, classes=classes, separated=separated, owners=owners)


def reference(multipoles, operators, classes, separated, owners):
    cells = multipoles.shape[1]
    blocks = cells // TB
    block_of = jnp.arange(cells, dtype=jnp.int32) // TB
    weight = separated[block_of][:, block_of]

    def per_class(k, total):
        moved = jnp.dot(operators[k], multipoles, preferred_element_type=jnp.float32).astype(jnp.bfloat16)
        pick = jnp.where((classes == k) & (weight == 1), 1.0, 0.0).astype(jnp.float32)
        return total + jnp.dot(moved.astype(jnp.float32), pick.T, precision=lax.Precision.HIGHEST, preferred_element_type=jnp.float32)

    local = lax.fori_loop(0, operators.shape[0], per_class, jnp.zeros((multipoles.shape[0], cells), jnp.float32))
    owner_rows = owners.reshape(blocks, TB)
    hit = (owner_rows[:, None, :] == jnp.arange(GROUP, dtype=jnp.int32)[None, :, None]).astype(jnp.int32)
    before = jnp.cumsum(hit, axis=2) - hit
    rank = jnp.sum(before * hit, axis=1)
    target = ((jnp.arange(blocks, dtype=jnp.int32)[:, None] * GROUP + owner_rows) * CAP + rank).reshape(-1)
    owned = jnp.zeros((multipoles.shape[0], blocks * GROUP * CAP), jnp.float32).at[:, target].set(local)
    return owned
```

```python
import functools

import jax
import jax.numpy as jnp
from jax import lax
from jax.experimental import pallas as pl
from jax.experimental.pallas import tpu as pltpu
from jax.sharding import PartitionSpec as P

MESH = pl.DeviceIdType.MESH
F32 = jnp.float32
BF16 = jnp.bfloat16


def split_rows(rows):
    first = (rows // 2 + 15) // 16 * 16
    return ((0, first), (first, rows - first))


def kernel(
    dims,
    mult_hbm,
    op_hbm,
    cls_hbm,
    sep_ref,
    own_ref,
    out_ref,
    gath,
    mult,
    ops,
    cls,
    pick,
    moved,
    acc,
    place,
    psend0,
    psend1,
    precv0,
    precv1,
    zsend0,
    zsend1,
    zrecv0,
    zrecv1,
    local_sem,
    g_send,
    g_recv,
    p_send,
    p_recv,
    z_send,
    z_recv,
):
    n_row, n_col, n_core, spread = dims
    rows, width = mult_hbm.shape
    count = op_hbm.shape[0]
    targets, sources = cls_hbm.shape
    slots = zsend0.shape[2]
    group = n_col * n_core
    row = lax.axis_index("row")
    col = lax.axis_index("col")
    core = lax.axis_index("cores")
    parts = split_rows(rows)
    psend, precv = (psend0, psend1), (precv0, precv1)
    zsend, zrecv = (zsend0, zsend1), (zrecv0, zrecv1)

    barrier = pltpu.get_barrier_semaphore()
    for d in range(1, n_row):
        pl.semaphore_signal(
            barrier, inc=1, device_id={"row": lax.rem(row + d, n_row)}, device_id_type=MESH
        )
    for d in range(1, n_col):
        pl.semaphore_signal(
            barrier, inc=1, device_id={"col": lax.rem(col + d, n_col)}, device_id_type=MESH
        )
    pl.semaphore_signal(barrier, inc=1, device_id={"cores": 1 - core}, device_id_type=MESH)

    cls_copy = pltpu.make_async_copy(cls_hbm, cls, local_sem.at[0])
    cls_copy.start()
    own_copy = pltpu.make_async_copy(mult_hbm, gath.at[row], local_sem.at[1])
    own_copy.start()
    op_copy = pltpu.make_async_copy(op_hbm, ops, local_sem.at[2])
    op_copy.start()

    pl.semaphore_wait(barrier, n_row - 1 + n_col - 1 + 1)

    gathers = []
    for d in range(1, n_row):
        copy = pltpu.make_async_remote_copy(
            src_ref=mult_hbm,
            dst_ref=gath.at[row],
            send_sem=g_send.at[d - 1],
            recv_sem=g_recv.at[d - 1],
            device_id={"row": lax.rem(row + d, n_row)},
            device_id_type=MESH,
        )
        copy.start()
        gathers.append(copy)

    cls_copy.wait()
    per = sources // spread
    for j in range(spread):
        flag = sep_ref[0, j]
        block = cls[:, j * per : (j + 1) * per]
        wanted = (block - core * count) * flag + (flag - 1)
        turned = wanted.astype(F32).T
        for k in range(count):
            pick[pl.ds(k * sources + j * per, per), :] = jnp.where(
                turned == float(k), 1.0, 0.0
            ).astype(BF16)

    owners = own_ref[...]
    ids = lax.broadcasted_iota(jnp.int32, (group, targets), 0)
    hit = jnp.where(ids == owners, 1.0, 0.0)
    upper = jnp.where(
        lax.broadcasted_iota(jnp.int32, (targets, targets), 0)
        < lax.broadcasted_iota(jnp.int32, (targets, targets), 1),
        1.0,
        0.0,
    ).astype(BF16)
    before = jnp.dot(hit.astype(BF16), upper, preferred_element_type=F32)
    rank = jnp.sum(before * hit, axis=0, keepdims=True)
    slot = lax.broadcasted_iota(jnp.int32, (slots, targets), 0).astype(F32)
    for c in range(n_col):
        mine = jnp.where(owners == c * n_core + core, rank, -1.0)
        place[:, c * slots : (c + 1) * slots] = jnp.where(slot == mine, 1.0, 0.0).T.astype(BF16)

    own_copy.wait()
    for copy in gathers:
        copy.wait()
    if width % 128 == 0:
        for r in range(n_row):
            mult[:, r * width : (r + 1) * width] = gath[r]
    else:
        mult[...] = jnp.concatenate([gath[r] for r in range(n_row)], axis=1)
    op_copy.wait()

    def translate(part):
        start, size = parts[part]

        @pl.loop(0, count, unroll=4)
        def _(k):
            at = pl.multiple_of(k * sources, sources)
            moved[part * parts[0][1] : part * parts[0][1] + size, pl.ds(at, sources)] = jnp.dot(
                ops[k, start : start + size, :], mult[...], preferred_element_type=F32
            ).astype(BF16)

    def collect(part):
        start, size = parts[part]
        chunk = 4 if count % 4 == 0 else 1
        acc[0:size, :] = jnp.zeros((size, targets), F32)

        @pl.loop(0, count // chunk)
        def _(g):
            at = pl.multiple_of(g * chunk * sources, chunk * sources)
            acc[0:size, :] += jnp.dot(
                moved[part * parts[0][1] : part * parts[0][1] + size, pl.ds(at, chunk * sources)],
                pick[pl.ds(at, chunk * sources), :],
                preferred_element_type=F32,
            )

    def pair_start(part):
        size = parts[part][1]
        psend[part][...] = acc[0:size, :].astype(BF16)
        copy = pltpu.make_async_remote_copy(
            src_ref=psend[part],
            dst_ref=precv[part],
            send_sem=p_send.at[part],
            recv_sem=p_recv.at[part],
            device_id={"cores": 1 - core},
            device_id_type=MESH,
        )
        copy.start()
        return copy

    def spread_start(part, pair):
        size = parts[part][1]
        pair.wait()
        both = (psend[part][...].astype(F32) + precv[part][...].astype(F32)).astype(BF16)
        if slots % 128 == 0:
            placed = jnp.dot(both, place[...], preferred_element_type=F32).astype(BF16)
            for c in range(n_col):
                zsend[part][c] = placed[:, c * slots : (c + 1) * slots]
        else:
            for c in range(n_col):
                zsend[part][c] = jnp.dot(
                    both, place[:, c * slots : (c + 1) * slots], preferred_element_type=F32
                ).astype(BF16)
        copies = []
        for d in range(1, n_col):
            to = lax.rem(col + d, n_col)
            copy = pltpu.make_async_remote_copy(
                src_ref=zsend[part].at[to],
                dst_ref=zrecv[part].at[d - 1],
                send_sem=z_send.at[part, d - 1],
                recv_sem=z_recv.at[part, d - 1],
                device_id={"col": to},
                device_id_type=MESH,
            )
            copy.start()
            copies.append(copy)
        return copies

    def finish(part, copies):
        start, size = parts[part]
        for copy in copies:
            copy.wait()
        total = zsend[part][col].astype(F32)
        for d in range(1, n_col):
            total += zrecv[part][d - 1].astype(F32)
        out_ref[start : start + size, :] = total

    translate(0)
    collect(0)
    pair0 = pair_start(0)
    translate(1)
    sends0 = spread_start(0, pair0)
    collect(1)
    pair1 = pair_start(1)
    sends1 = spread_start(1, pair1)
    finish(0, sends0)
    finish(1, sends1)


def solution(mesh):
    n_row, n_col, n_core = mesh.shape["row"], mesh.shape["col"], mesh.shape["cores"]

    def shards(multipoles, operators, classes, separated, owners):
        rows, width = multipoles.shape
        count = operators.shape[0]
        targets, sources = classes.shape
        slots = 2 * targets // (n_col * n_core)
        sizes = [size for _, size in split_rows(rows)]
        top = sizes[0] * 2
        hbm = pl.BlockSpec(memory_space=pl.ANY)
        dma = pltpu.SemaphoreType.DMA
        return pl.pallas_call(
            functools.partial(kernel, (n_row, n_col, n_core, separated.shape[1])),
            out_shape=jax.ShapeDtypeStruct((rows, slots), F32),
            in_specs=[
                hbm,
                hbm,
                hbm,
                pl.BlockSpec(memory_space=pltpu.SMEM),
                pl.BlockSpec(memory_space=pltpu.VMEM),
            ],
            out_specs=pl.BlockSpec(memory_space=pltpu.VMEM),
            scratch_shapes=[
                pltpu.VMEM((n_row, rows, width), BF16),
                pltpu.VMEM((rows, sources), BF16),
                pltpu.VMEM((count, rows, rows), BF16),
                pltpu.VMEM((targets, sources), jnp.int32),
                pltpu.VMEM((count * sources, targets), BF16),
                pltpu.VMEM((top, count * sources), BF16),
                pltpu.VMEM((sizes[0], targets), F32),
                pltpu.VMEM((targets, n_col * slots), BF16),
            ]
            + [pltpu.VMEM((size, targets), BF16) for size in sizes]
            + [pltpu.VMEM((size, targets), BF16) for size in sizes]
            + [pltpu.VMEM((n_col, size, slots), BF16) for size in sizes]
            + [pltpu.VMEM((n_col - 1, size, slots), BF16) for size in sizes]
            + [
                dma((3,)),
                dma((n_row - 1,)),
                dma((n_row - 1,)),
                dma((2,)),
                dma((2,)),
                dma((2, n_col - 1)),
                dma((2, n_col - 1)),
            ],
            compiler_params=pltpu.CompilerParams(
                collective_id=0, has_side_effects=True, vmem_limit_bytes=60 * 1024 * 1024
            ),
        )(multipoles, operators, classes, separated, owners.reshape(1, targets))

    return jax.shard_map(
        shards,
        mesh=mesh,
        in_specs=(
            P(None, ("col", "row")),
            P("cores", None, None),
            P("row", "col"),
            P("row", "col"),
            P("row"),
        ),
        out_specs=P(None, ("row", "col", "cores")),
        check_vma=False,
    )
```
